128 devices in a mesh: rep: 16 (over x, y), exp: 8 (over z, core).
Axes of the slice: x: 4, y: 4, z: 4, core: 2. Of those that a mesh axis runs over, the one named last changes fastest.
Arguments:
- hidden: bfloat16 [16384, 4096], P(('rep', 'exp')), may hold values from -6 to 6
- parents: int32 [16384], P(('rep', 'exp')), may hold values from 0 to 1023
- routes: int32 [16384, 8], P(('rep', 'exp')), may hold values from 0 to 127, all different within a row; in each aligned block of 128 rows (0 to 127, 128 to 255, ...) at most 10 rows name the same one
- gates: float32 [16384, 8], P(('rep', 'exp')), may hold values from 0.05 to 1
- counts: int32 [128], P(('rep', 'exp')), may hold values from 64 to 128, as said below
- norm_gain: float32 [4096], replicated, may hold values from 0.1 to 1.9
- w_gate: bfloat16 [128, 4096, 768], P(('rep', 'exp')), may hold values from -0.09375 to 0.09375
- w_up: bfloat16 [128, 4096, 768], P(('rep', 'exp')), may hold values from -0.09375 to 0.09375
- w_down: bfloat16 [128, 768, 4096], P(('rep', 'exp')), may hold values from -0.21875 to 0.21875
Outputs:
- mixed: bfloat16 [16384, 4096], P(('rep', 'exp'))
The draws below stay inside these ranges and needn't reach their ends.
Inputs may be any that keep to these rules, and one draw needn't show every extreme that they name: `routes`: in the rows of one device no expert is named more than 10 times. `counts`: some device has all of its rows live.
All inputs are finite; a program needn't handle non-finite values.
Results may differ from the reference program's by a relative error of at most 0.0071.
Values may be sent and summed in bfloat16 or wider, within the bound.
A program may use at most 128 MiB of HBM per device.

```python
import math
import jax
import jax.numpy as jnp
import numpy as np
from jax import lax

D = 4096
FFW = 768
TOP = 8
ROWS_DEV = 128
EXPERTS = 128
BLOCKS = 128
MICRO = 1024
ROWS = 16384
CAP = 10
N_EXP = 8


def draw_counts(key, part):
    base = jax.random.randint(key, (BLOCKS,), ROWS_DEV // 2, ROWS_DEV + 1)
    chosen = jax.random.randint(jax.random.fold_in(key, 7), (), 0, BLOCKS)
    return jnp.where(jnp.arange(BLOCKS) == chosen, ROWS_DEV, base).astype(jnp.int32)


def place_ends(array, own_key, low, high):
    extent = array.shape
    index_at = [jax.random.randint(jax.random.fold_in(own_key, axis), (), 0, extent[axis]) for axis in range(len(extent))]
    array = array.at[tuple(index_at)].set(low)
    longest = extent.index(max(extent))
    index_at[longest] = (index_at[longest] + 1) % extent[longest]
    return array.at[tuple(index_at)].set(high)


def levels(stream_key, extent, split, least, largest):
    factor_of, own = 1.0, jax.random.fold_in(stream_key, 6)
    for dim, blocks in split:
        draws = jnp.exp(jax.random.uniform(jax.random.fold_in(own, dim), (blocks,), jnp.float32, least / len(split), largest / len(split)))
        factor_of = factor_of * jnp.repeat(draws, extent[dim] // blocks).reshape([-1 if axis == dim else 1 for axis in range(len(extent))])
    return factor_of


def shared_out(stream_key, own, number, rows, number_of, top, most, skew):
    sequence = jax.random.permutation(stream_key, number_of)
    packed, ordinary = load_shares(number_of, rows * top, most, skew, True), load_shares(number_of, rows * top, most, skew, False)
    places = jnp.arange(number_of)

    def named(lengths, rotation):
        used = int((lengths > 0).sum())
        fixed = max(1, used // 4)
        moved = fixed + (places - fixed + rotation * (used - fixed)) % max(1, number_of - fixed)
        return jnp.zeros((number_of,), jnp.int32).at[sequence[jnp.where(places < fixed, places, moved)]].set(jnp.asarray(lengths, jnp.int32))

    lengths = jnp.where(number % 4 == 0, named(packed, number // 4), named(ordinary, number - number // 4 - 1))
    mixed = jax.random.permutation(jax.random.fold_in(own, 3), number_of)
    source_of, sink = mixed[0:number_of // 2 * 2:2], mixed[1:number_of // 2 * 2:2]
    slack = jnp.minimum(lengths[source_of] - 1, most - lengths[sink]) // 2
    slack = jnp.where((source_of == sequence[0]) | (sink == sequence[0]) | (lengths[sink] == 0), 0, jnp.maximum(slack, 0))
    moved = jax.random.randint(jax.random.fold_in(own, 4), (number_of // 2,), 0, 1 << 20) % (slack + 1)
    lengths = lengths.at[source_of].add(-moved).at[sink].add(moved)
    items = jnp.searchsorted(jnp.cumsum(lengths), jnp.arange(rows * top), side="right").astype(jnp.int32)
    table = items.reshape(top, rows).T
    table = table[jax.random.permutation(jax.random.fold_in(own, 1), rows)]
    rotation = jax.random.randint(jax.random.fold_in(own, 2), (rows, 1), 0, top)
    return jnp.take_along_axis(table, (jnp.arange(top)[None, :] + rotation) % top, axis=1)


def load_shares(count, total, bound, skew, full):
    portions = [(1 << 20) // math.isqrt(standing ** skew) + 1 for standing in range(1, count + 1)]
    largest = bound if full else min(bound, max(-(-total // count), total * portions[0] // sum(portions)))
    least = 1 if total - largest >= count - 1 else 0
    given, spare = [largest] + [least] * (count - 1), total - largest - least * (count - 1)
    while spare > 0:
        movable = [i for i in range(1, count) if given[i] < largest] or [i for i in range(1, count) if given[i] < bound]
        mass, budget = sum([portions[i] for i in movable]), spare
        for i in movable:
            more = min(bound - given[i], max(1, budget * portions[i] // mass), spare)
            given[i] = given[i] + more
            spare = spare - more
    return np.array(given)


def scatter_about(key, shape, deviation, bound, split=(), kind=jnp.bfloat16):
    array = deviation * jax.random.normal(key, shape, jnp.float32)
    if split:
        array = array * levels(key, shape, split, -0.22, 0.18)
    return jnp.clip(array, -bound, bound).astype(kind)


def setup_inputs(seed: int = 0) -> dict:
    seeds = jax.random.split(jax.random.key(seed), 10)
    hidden = scatter_about(seeds[0], (ROWS, D), 1.0, 6.0, ((0, 128),))
    parents = place_ends(jax.random.randint(seeds[1], (ROWS,), 0, MICRO), jax.random.fold_in(seeds[1], 1), 0, MICRO - 1).astype(jnp.int32)
    routes_keys = jax.random.split(jax.random.fold_in(seeds[2], 1), ROWS // ROWS_DEV)
    routes_turns = jax.random.permutation(jax.random.fold_in(seeds[2], 3), ROWS // ROWS_DEV)
    routes = jax.vmap(lambda own, number: shared_out(jax.random.fold_in(seeds[2], 2), own, number, ROWS_DEV, EXPERTS, TOP, CAP, 1))(routes_keys, routes_turns).reshape((ROWS, TOP))
    gates = jnp.clip(0.05 + 0.95 * jax.random.uniform(seeds[3], (ROWS, TOP), jnp.float32) ** levels(seeds[3], (ROWS, TOP), ((0, 128),), -0.2, 0.2), 0.05, 1.0)
    counts = draw_counts(jax.random.fold_in(seeds[9], 71), 0)
    norm_gain = jnp.clip(1.0 + 0.18 * jax.random.normal(seeds[5], (D,), jnp.float32), 0.1, 1.9)
    w_gate = scatter_about(seeds[6], (EXPERTS, D, FFW), D ** -0.5, 0.09375, ((0, 128),))
    w_up = scatter_about(seeds[7], (EXPERTS, D, FFW), D ** -0.5, 0.09375, ((0, 128),))
    w_down = scatter_about(seeds[8], (EXPERTS, FFW, D), FFW ** -0.5, 0.21875, ((0, 128),))
    return {"hidden": hidden, "parents": parents, "routes": routes, "gates": gates, "counts": counts, "norm_gain": norm_gain, "w_gate": w_gate, "w_up": w_up, "w_down": w_down}


def reference(hidden, parents, routes, gates, counts, norm_gain, w_gate, w_up, w_down):
    micro = ROWS_DEV * N_EXP
    total_rows = hidden.shape[0]
    order = jnp.arange(total_rows, dtype=jnp.int32)
    source_row = (order // micro * micro + parents).astype(jnp.int32)
    picked = jnp.take(hidden, source_row, axis=0).astype(jnp.float32)
    scale = lax.rsqrt(lax.optimization_barrier(jnp.mean(picked * picked, axis=1, keepdims=True)) + 1e-06)
    normed = (picked * scale * norm_gain).astype(jnp.bfloat16)
    live = order % ROWS_DEV < jnp.take(counts, order // ROWS_DEV)
    weights = gates / lax.optimization_barrier(jnp.sum(gates, axis=1, keepdims=True)) * live[:, None].astype(gates.dtype)
    flat = routes.reshape(-1)
    slots = BLOCKS * CAP
    live_slot = jnp.repeat(live, TOP)
    onehot = ((flat[:, None] == jnp.arange(EXPERTS, dtype=jnp.int32)[None, :]) & live_slot[:, None]).astype(jnp.int32)
    before = jnp.cumsum(onehot, axis=0) - onehot
    rank = lax.optimization_barrier(jnp.sum(before * onehot, axis=1)).astype(jnp.int32)
    position = jnp.where(live_slot, flat * slots + rank, EXPERTS * slots).astype(jnp.int32)
    sentinel = total_rows * TOP
    table = jnp.full((EXPERTS * slots,), sentinel, jnp.int32)
    table = table.at[position].set(jnp.arange(sentinel, dtype=jnp.int32), mode='drop').reshape(EXPERTS, slots)
    flat_weights = weights.reshape(-1)

    def one_expert(accum, item):
        entry, gate_part, up_part, down_part = item
        valid = entry < sentinel
        safe = jnp.minimum(entry, sentinel - 1).astype(jnp.int32)
        rows_in = jnp.take(normed, safe // TOP, axis=0).astype(jnp.float32)
        gate_val = jnp.dot(rows_in, gate_part.astype(jnp.float32), precision=lax.Precision.HIGHEST)
        up_val = jnp.dot(rows_in, up_part.astype(jnp.float32), precision=lax.Precision.HIGHEST)
        act = (jax.nn.silu(gate_val) * up_val).astype(jnp.bfloat16)
        result = jnp.dot(act.astype(jnp.float32), down_part.astype(jnp.float32), precision=lax.Precision.HIGHEST).astype(jnp.bfloat16)
        share = jnp.where(valid, jnp.take(flat_weights, safe), jnp.zeros((), flat_weights.dtype))
        accum = accum.at[safe // TOP].add(share[:, None] * result.astype(jnp.float32))
        return (accum, None)
    mixed, _ = lax.scan(one_expert, jnp.zeros((total_rows, D), jnp.float32), (table, w_gate, w_up, w_down))
    return mixed.astype(jnp.bfloat16)
```

```python
import jax
import jax.numpy as jnp
from jax import lax
from jax.experimental import pallas as pl
from jax.experimental.pallas import tpu as pltpu
from jax.sharding import PartitionSpec as P
import functools

MESH = pl.DeviceIdType.MESH


def exchange_kernel(n_rep, n_exp, x_ref, o_ref, send_sem, recv_sem, local_sem):
    n = n_rep * n_exp
    me = lax.axis_index("rep") * n_exp + lax.axis_index("exp")
    barrier = pltpu.get_barrier_semaphore()

    def greet(s, carry):
        d = lax.rem(me + s, n)
        pl.semaphore_signal(barrier, inc=1, device_id=(d // n_exp, d % n_exp), device_id_type=MESH)
        return carry

    lax.fori_loop(1, n, greet, 0)
    pl.semaphore_wait(barrier, n - 1)
    own = pltpu.make_async_copy(x_ref.at[me], o_ref.at[me], local_sem)
    own.start()

    def send(s, carry):
        d = lax.rem(me + s, n)
        pltpu.make_async_remote_copy(
            src_ref=x_ref.at[d], dst_ref=o_ref.at[me], send_sem=send_sem, recv_sem=recv_sem,
            device_id=(d // n_exp, d % n_exp), device_id_type=MESH,
        ).start()
        return carry

    lax.fori_loop(1, n, send, 0)
    own.wait()
    whole = pltpu.make_async_remote_copy(
        src_ref=x_ref.at[pl.ds(0, n - 1)], dst_ref=o_ref.at[pl.ds(0, n - 1)], send_sem=send_sem,
        recv_sem=recv_sem, device_id=(0, 0), device_id_type=MESH,
    )
    whole.wait_send()
    whole.wait_recv()


def exchange(x, ident):
    n_rep = lax.axis_size("rep")
    n_exp = lax.axis_size("exp")
    return pl.pallas_call(
        functools.partial(exchange_kernel, n_rep, n_exp),
        out_shape=jax.ShapeDtypeStruct(x.shape, x.dtype),
        in_specs=[pl.BlockSpec(memory_space=pl.ANY)],
        out_specs=pl.BlockSpec(memory_space=pl.ANY),
        scratch_shapes=[pltpu.SemaphoreType.DMA, pltpu.SemaphoreType.DMA, pltpu.SemaphoreType.DMA],
        compiler_params=pltpu.CompilerParams(collective_id=ident, has_side_effects=True),
        name=f"exchange{ident}",
    )(x)


def run_expert(arrived, w_gate, w_up, w_down):
    gate_val = jnp.dot(arrived, w_gate[0], preferred_element_type=jnp.float32)
    up_val = jnp.dot(arrived, w_up[0], preferred_element_type=jnp.float32)
    act = (jax.nn.silu(gate_val) * up_val).astype(jnp.bfloat16)
    return jnp.dot(act, w_down[0], preferred_element_type=jnp.float32).astype(jnp.bfloat16)


def shards(hidden, parents, routes, gates, counts, norm_gain, w_gate, w_up, w_down):
    rows = hidden.shape[0]
    width = hidden.shape[1]
    top = routes.shape[1]
    n_rep = lax.axis_size("rep")
    n_exp = lax.axis_size("exp")
    n_dev = n_rep * n_exp
    cap = rows * top // n_dev + 2
    group = lax.all_gather(hidden, "exp", axis=0, tiled=True)
    picked = jnp.take(group, parents, axis=0).astype(jnp.float32)
    scale = lax.rsqrt(jnp.mean(picked * picked, axis=1, keepdims=True) + 1e-06)
    normed = (picked * scale * norm_gain).astype(jnp.bfloat16)
    live = jnp.arange(rows, dtype=jnp.int32) < counts[0]
    weights = gates / jnp.sum(gates, axis=1, keepdims=True) * live[:, None].astype(jnp.float32)
    flat = routes.reshape(-1)
    live_slot = jnp.repeat(live, top)
    onehot = (
        (flat[:, None] == jnp.arange(n_dev, dtype=jnp.int32)[None, :]) & live_slot[:, None]
    ).astype(jnp.int32)
    before = jnp.cumsum(onehot, axis=0) - onehot
    rank = jnp.sum(before * onehot, axis=1)
    position = jnp.where(live_slot, flat * cap + rank, n_dev * cap)
    row_of_slot = jnp.arange(rows * top, dtype=jnp.int32) // top
    source = jnp.zeros((n_dev * cap,), jnp.int32).at[position].set(row_of_slot, mode="drop")
    filled = jnp.zeros((n_dev * cap,), jnp.bool_).at[position].set(True, mode="drop")
    outgoing = jnp.where(
        filled[:, None], jnp.take(normed, source, axis=0), jnp.zeros((), jnp.bfloat16)
    )
    arrived = exchange(outgoing.reshape(n_dev, cap, width), 0).reshape(n_dev * cap, width)
    results = run_expert(arrived, w_gate, w_up, w_down)
    returned = exchange(results.reshape(n_dev, cap, width), 1).reshape(n_dev * cap, width)
    safe = jnp.minimum(position, n_dev * cap - 1)
    collected = jnp.take(returned, safe, axis=0).reshape(rows, top, width)
    mixed = jnp.zeros((rows, width), jnp.float32)
    for slot in range(top):
        mixed = mixed + weights[:, slot : slot + 1] * collected[:, slot].astype(jnp.float32)
    return mixed.astype(jnp.bfloat16)


def solution(mesh):
    placed = (
        P(("rep", "exp"), None),
        P(("rep", "exp")),
        P(("rep", "exp"), None),
        P(("rep", "exp"), None),
        P(("rep", "exp")),
        P(),
        P(("rep", "exp"), None, None),
        P(("rep", "exp"), None, None),
        P(("rep", "exp"), None, None),
    )
    return jax.shard_map(
        shards, mesh=mesh, in_specs=placed, out_specs=P(("rep", "exp"), None), check_vma=False
    )
```

```python
import jax
import jax.numpy as jnp
from jax import lax
from jax.sharding import PartitionSpec as P


def run_expert(arrived, w_gate, w_up, w_down):
    gate_val = jnp.dot(arrived, w_gate[0], preferred_element_type=jnp.float32)
    up_val = jnp.dot(arrived, w_up[0], preferred_element_type=jnp.float32)
    act = (jax.nn.silu(gate_val) * up_val).astype(jnp.bfloat16)
    return jnp.dot(act, w_down[0], preferred_element_type=jnp.float32).astype(jnp.bfloat16)


def shards(hidden, parents, routes, gates, counts, norm_gain, w_gate, w_up, w_down):
    rows = hidden.shape[0]
    width = hidden.shape[1]
    top = routes.shape[1]
    n_rep = lax.axis_size("rep")
    n_exp = lax.axis_size("exp")
    n_dev = n_rep * n_exp
    cap = rows * top // n_dev + 2
    column = lax.axis_index("exp")
    micro = rows * n_exp
    per_expert = cap * n_exp
    slots = n_rep * per_expert

    live = jnp.arange(rows, dtype=jnp.int32) < counts[0]
    weights = gates / jnp.sum(gates, axis=1, keepdims=True) * live[:, None].astype(jnp.float32)
    flat = routes.reshape(-1)
    live_slot = jnp.repeat(live, top)
    onehot = (
        (flat[:, None] == jnp.arange(n_dev, dtype=jnp.int32)[None, :]) & live_slot[:, None]
    ).astype(jnp.int32)
    before = jnp.cumsum(onehot, axis=0) - onehot
    rank = jnp.sum(before * onehot, axis=1)
    code = jnp.where(live_slot, flat, -1)
    ints = jnp.concatenate(
        [code.reshape(rows, top), rank.reshape(rows, top), parents[:, None]], axis=1
    )

    group = lax.all_gather(hidden, "exp", axis=0, tiled=True)
    ints_all = lax.all_gather(ints, "exp", axis=0, tiled=True)
    w_all = lax.all_gather(weights, "exp", axis=0, tiled=True)

    code_all = ints_all[:, :top]
    rank_all = ints_all[:, top : 2 * top]
    parent_all = ints_all[:, 2 * top]
    mine = (code_all >= 0) & (code_all % n_exp == column)
    owner = (jnp.arange(micro, dtype=jnp.int32) // rows)[:, None]
    dest = (code_all // n_exp) * per_expert + owner * cap + rank_all
    dest = jnp.where(mine, dest, slots).reshape(-1)
    row_id = jnp.broadcast_to(jnp.arange(micro, dtype=jnp.int32)[:, None], (micro, top)).reshape(-1)
    src_row = jnp.zeros((slots,), jnp.int32).at[dest].set(row_id, mode="drop")
    filled = jnp.zeros((slots,), jnp.bool_).at[dest].set(True, mode="drop")
    slot_w = jnp.zeros((slots,), jnp.float32).at[dest].set(w_all.reshape(-1), mode="drop")

    picked = jnp.take(group, jnp.take(parent_all, src_row), axis=0).astype(jnp.float32)
    scale = lax.rsqrt(jnp.mean(picked * picked, axis=1, keepdims=True) + 1e-06)
    normed = (picked * scale * norm_gain).astype(jnp.bfloat16)
    outgoing = jnp.where(filled[:, None], normed, jnp.zeros((), jnp.bfloat16))

    arrived = lax.all_to_all(outgoing, "rep", split_axis=0, concat_axis=0, tiled=True)
    results = run_expert(arrived, w_gate, w_up, w_down)
    returned = lax.all_to_all(results, "rep", split_axis=0, concat_axis=0, tiled=True)

    contrib = slot_w[:, None] * returned.astype(jnp.float32)
    target = jnp.where(filled, src_row, micro)
    partial = jnp.zeros((micro, width), jnp.float32).at[target].add(contrib, mode="drop")
    mixed = lax.psum_scatter(partial.astype(jnp.bfloat16), "exp", scatter_dimension=0, tiled=True)
    return mixed


def solution(mesh):
    placed = (
        P(("rep", "exp"), None),
        P(("rep", "exp")),
        P(("rep", "exp"), None),
        P(("rep", "exp"), None),
        P(("rep", "exp")),
        P(),
        P(("rep", "exp"), None, None),
        P(("rep", "exp"), None, None),
        P(("rep", "exp"), None, None),
    )
    return jax.shard_map(
        shards, mesh=mesh, in_specs=placed, out_specs=P(("rep", "exp"), None), check_vma=False
    )
```

```python
import jax
import jax.numpy as jnp
from jax import lax
from jax.sharding import PartitionSpec as P


def run_expert(arrived, w_gate, w_up, w_down):
    gate_val = jnp.dot(arrived, w_gate[0], preferred_element_type=jnp.float32)
    up_val = jnp.dot(arrived, w_up[0], preferred_element_type=jnp.float32)
    act = (jax.nn.silu(gate_val) * up_val).astype(jnp.bfloat16)
    return jnp.dot(act, w_down[0], preferred_element_type=jnp.float32).astype(jnp.bfloat16)


def shards(hidden, parents, routes, gates, counts, norm_gain, w_gate, w_up, w_down):
    rows = hidden.shape[0]
    width = hidden.shape[1]
    top = routes.shape[1]
    n_rep = lax.axis_size("rep")
    n_exp = lax.axis_size("exp")
    n_dev = n_rep * n_exp
    cap = rows * top // n_dev + 2
    column = lax.axis_index("exp")
    micro = rows * n_exp
    per_expert = cap * n_exp
    slots = n_rep * per_expert

    live = jnp.arange(rows, dtype=jnp.int32) < counts[0]
    weights = gates / jnp.sum(gates, axis=1, keepdims=True) * live[:, None].astype(jnp.float32)
    flat = routes.reshape(-1)
    live_slot = jnp.repeat(live, top)
    onehot = (
        (flat[:, None] == jnp.arange(n_dev, dtype=jnp.int32)[None, :]) & live_slot[:, None]
    ).astype(jnp.int32)
    before = jnp.cumsum(onehot, axis=0) - onehot
    rank = jnp.sum(before * onehot, axis=1)
    position = jnp.where(live_slot, flat * cap + rank, n_dev * cap)
    slot_row = jnp.arange(rows * top, dtype=jnp.int32) // top
    match = position[:, None] == jnp.arange(n_dev * cap, dtype=jnp.int32)[None, :]
    filled_here = jnp.any(match, axis=0)
    row_here = jnp.sum(jnp.where(match, slot_row[:, None], 0), axis=0)
    parent_here = jnp.sum(jnp.where(match, jnp.take(parents, slot_row)[:, None], 0), axis=0)
    w_here = jnp.sum(jnp.where(match, weights.reshape(-1)[:, None], 0.0), axis=0)
    table = jnp.stack(
        [
            jnp.where(filled_here, row_here, -1).astype(jnp.float32),
            parent_here.astype(jnp.float32),
            w_here,
        ],
        axis=1,
    )

    group = lax.all_gather(hidden, "exp", axis=0, tiled=True)
    table_all = lax.all_gather(table, "exp", axis=0, tiled=False)
    table_all = table_all.reshape(n_exp, n_rep, n_exp, cap, 3)
    table_col = lax.dynamic_index_in_dim(table_all, column, axis=2, keepdims=False)
    table_col = jnp.transpose(table_col, (1, 0, 2, 3))
    row_tbl = table_col[..., 0].astype(jnp.int32)
    src_row = table_col[..., 1].astype(jnp.int32).reshape(-1)
    w_tbl = table_col[..., 2]
    filled = (row_tbl >= 0).reshape(-1)

    picked = jnp.take(group, src_row, axis=0).astype(jnp.float32)
    scale = lax.rsqrt(jnp.mean(picked * picked, axis=1, keepdims=True) + 1e-06)
    normed = (picked * scale * norm_gain).astype(jnp.bfloat16)
    outgoing = jnp.where(filled[:, None], normed, jnp.zeros((), jnp.bfloat16))

    arrived = lax.all_to_all(outgoing, "rep", split_axis=0, concat_axis=0, tiled=True)
    results = run_expert(arrived, w_gate, w_up, w_down)
    returned = lax.all_to_all(results, "rep", split_axis=0, concat_axis=0, tiled=True)

    returned = returned.reshape(n_rep, n_exp, cap, width)
    pick = row_tbl[None] == jnp.arange(rows, dtype=jnp.int32)[:, None, None, None]
    mix = jnp.transpose(jnp.where(pick, w_tbl[None], 0.0), (2, 0, 1, 3))
    mix_hi = mix.astype(jnp.bfloat16)
    mix_lo = (mix - mix_hi.astype(jnp.float32)).astype(jnp.bfloat16)
    partial = jnp.einsum("drec,edcw->drw", mix_hi, returned, preferred_element_type=jnp.float32)
    partial = partial + jnp.einsum(
        "drec,edcw->drw", mix_lo, returned, preferred_element_type=jnp.float32
    )
    partial = partial.reshape(micro, width)
    mixed = lax.psum_scatter(partial.astype(jnp.bfloat16), "exp", scatter_dimension=0, tiled=True)
    return mixed


def solution(mesh):
    placed = (
        P(("rep", "exp"), None),
        P(("rep", "exp")),
        P(("rep", "exp"), None),
        P(("rep", "exp"), None),
        P(("rep", "exp")),
        P(),
        P(("rep", "exp"), None, None),
        P(("rep", "exp"), None, None),
        P(("rep", "exp"), None, None),
    )
    return jax.shard_map(
        shards, mesh=mesh, in_specs=placed, out_specs=P(("rep", "exp"), None), check_vma=False
    )
```

```python
import jax
import jax.numpy as jnp
from jax import lax
from jax.sharding import PartitionSpec as P


def run_expert(arrived, w_gate, w_up, w_down):
    gate_val = jnp.dot(arrived, w_gate[0], preferred_element_type=jnp.float32)
    up_val = jnp.dot(arrived, w_up[0], preferred_element_type=jnp.float32)
    act = (jax.nn.silu(gate_val) * up_val).astype(jnp.bfloat16)
    return jnp.dot(act, w_down[0], preferred_element_type=jnp.float32).astype(jnp.bfloat16)


def shards(hidden, parents, routes, gates, counts, norm_gain, w_gate, w_up, w_down):
    rows = hidden.shape[0]
    width = hidden.shape[1]
    top = routes.shape[1]
    n_rep = lax.axis_size("rep")
    n_exp = lax.axis_size("exp")
    n_dev = n_rep * n_exp
    cap = rows * top // n_dev + 2
    column = lax.axis_index("exp")
    micro = rows * n_exp
    per_expert = cap * n_exp
    slots = n_rep * per_expert

    live = jnp.arange(rows, dtype=jnp.int32) < counts[0]
    weights = gates / jnp.sum(gates, axis=1, keepdims=True) * live[:, None].astype(jnp.float32)
    flat = routes.reshape(-1)
    live_slot = jnp.repeat(live, top)
    onehot = (
        (flat[:, None] == jnp.arange(n_dev, dtype=jnp.int32)[None, :]) & live_slot[:, None]
    ).astype(jnp.int32)
    before = jnp.cumsum(onehot, axis=0) - onehot
    rank = jnp.sum(before * onehot, axis=1)
    position = jnp.where(live_slot, flat * cap + rank, n_dev * cap)
    slot_row = jnp.arange(rows * top, dtype=jnp.int32) // top
    match = position[:, None] == jnp.arange(n_dev * cap, dtype=jnp.int32)[None, :]
    filled_here = jnp.any(match, axis=0)
    row_here = jnp.sum(jnp.where(match, slot_row[:, None], 0), axis=0)
    parent_here = jnp.sum(jnp.where(match, jnp.repeat(parents, top)[:, None], 0), axis=0)
    w_here = jnp.sum(jnp.where(match, weights.reshape(-1)[:, None], 0.0), axis=0)
    table = jnp.stack(
        [
            jnp.where(filled_here, row_here, -1).astype(jnp.float32),
            parent_here.astype(jnp.float32),
            w_here,
        ],
        axis=1,
    )

    group = lax.all_gather(hidden, "exp", axis=0, tiled=True)
    table_all = lax.all_gather(table, "exp", axis=0, tiled=False)
    table_all = table_all.reshape(n_exp, n_rep, n_exp, cap, 3)
    table_col = lax.dynamic_index_in_dim(table_all, column, axis=2, keepdims=False)
    table_col = jnp.transpose(table_col, (1, 0, 2, 3))
    row_tbl = table_col[..., 0].astype(jnp.int32)
    src_row = table_col[..., 1].astype(jnp.int32).reshape(-1)
    w_tbl = table_col[..., 2]
    filled = (row_tbl >= 0).reshape(-1)

    picked = jnp.take(group, src_row, axis=0).astype(jnp.float32)
    scale = lax.rsqrt(jnp.mean(picked * picked, axis=1, keepdims=True) + 1e-06)
    normed = (picked * scale * norm_gain).astype(jnp.bfloat16)
    outgoing = jnp.where(filled[:, None], normed, jnp.zeros((), jnp.bfloat16))

    arrived = lax.all_to_all(outgoing, "rep", split_axis=0, concat_axis=0, tiled=True)
    results = run_expert(arrived, w_gate, w_up, w_down)
    returned = lax.all_to_all(results, "rep", split_axis=0, concat_axis=0, tiled=True)
    returned = returned.reshape(n_rep, n_exp, cap, width)
    after = (returned[0, 0, 0, 0] * 0).astype(jnp.int32)
    pick = (row_tbl + after)[None] == jnp.arange(rows, dtype=jnp.int32)[:, None, None, None]
    mix = jnp.transpose(jnp.where(pick, (w_tbl + after.astype(jnp.float32))[None], 0.0), (2, 0, 1, 3))
    mix_hi = mix.astype(jnp.bfloat16)
    mix_lo = (mix - mix_hi.astype(jnp.float32)).astype(jnp.bfloat16)
    partial = jnp.einsum("drec,edcw->drw", mix_hi, returned, preferred_element_type=jnp.float32)
    partial = partial + jnp.einsum(
        "drec,edcw->drw", mix_lo, returned, preferred_element_type=jnp.float32
    )
    partial = partial.reshape(micro, width)
    mixed = lax.psum_scatter(partial.astype(jnp.bfloat16), "exp", scatter_dimension=0, tiled=True)
    return mixed


def solution(mesh):
    placed = (
        P(("rep", "exp"), None),
        P(("rep", "exp")),
        P(("rep", "exp"), None),
        P(("rep", "exp"), None),
        P(("rep", "exp")),
        P(),
        P(("rep", "exp"), None, None),
        P(("rep", "exp"), None, None),
        P(("rep", "exp"), None, None),
    )
    return jax.shard_map(
        shards, mesh=mesh, in_specs=placed, out_specs=P(("rep", "exp"), None), check_vma=False
    )
```

```python
import jax
import jax.numpy as jnp
from jax import lax
from jax.sharding import PartitionSpec as P


def run_expert(arrived, w_gate, w_up, w_down):
    gate_val = jnp.dot(arrived, w_gate[0], preferred_element_type=jnp.float32)
    up_val = jnp.dot(arrived, w_up[0], preferred_element_type=jnp.float32)
    act = (jax.nn.silu(gate_val) * up_val).astype(jnp.bfloat16)
    return jnp.dot(act, w_down[0], preferred_element_type=jnp.float32).astype(jnp.bfloat16)


def shards(hidden, parents, routes, gates, counts, norm_gain, w_gate, w_up, w_down):
    rows = hidden.shape[0]
    width = hidden.shape[1]
    top = routes.shape[1]
    n_rep = lax.axis_size("rep")
    n_exp = lax.axis_size("exp")
    n_dev = n_rep * n_exp
    cap = rows * top // n_dev + 2
    column = lax.axis_index("exp")
    micro = rows * n_exp
    per_expert = cap * n_exp
    slots = n_rep * per_expert

    live = jnp.arange(rows, dtype=jnp.int32) < counts[0]
    weights = gates / jnp.sum(gates, axis=1, keepdims=True) * live[:, None].astype(jnp.float32)
    flat = routes.reshape(-1)
    live_slot = jnp.repeat(live, top)
    onehot = (
        (flat[:, None] == jnp.arange(n_dev, dtype=jnp.int32)[None, :]) & live_slot[:, None]
    ).astype(jnp.int32)
    before = jnp.cumsum(onehot, axis=0) - onehot
    rank = jnp.sum(before * onehot, axis=1)
    position = jnp.where(live_slot, flat * cap + rank, n_dev * cap)
    slot_row = jnp.arange(rows * top, dtype=jnp.int32) // top
    match = position[:, None] == jnp.arange(n_dev * cap, dtype=jnp.int32)[None, :]
    filled_here = jnp.any(match, axis=0)
    row_here = jnp.sum(jnp.where(match, slot_row[:, None], 0), axis=0)
    parent_here = jnp.sum(jnp.where(match, jnp.repeat(parents, top)[:, None], 0), axis=0)
    w_here = jnp.sum(jnp.where(match, weights.reshape(-1)[:, None], 0.0), axis=0)
    table = jnp.stack(
        [
            jnp.where(filled_here, column * rows + row_here, -1).astype(jnp.float32),
            parent_here.astype(jnp.float32),
            w_here,
        ],
        axis=1,
    )

    own = hidden.astype(jnp.float32)
    own_scale = lax.rsqrt(jnp.mean(own * own, axis=1, keepdims=True) + 1e-06)
    normed = (own * own_scale * norm_gain).astype(jnp.bfloat16)
    group = lax.all_gather(normed, "exp", axis=0, tiled=True)
    table_all = lax.all_gather(table, "exp", axis=0, tiled=False)
    table_all = table_all.reshape(n_exp, n_rep, n_exp, cap, 3)
    table_col = lax.dynamic_index_in_dim(table_all, column, axis=2, keepdims=False)
    table_col = jnp.transpose(table_col, (1, 0, 2, 3))
    row_tbl = table_col[..., 0].astype(jnp.int32)
    src_row = table_col[..., 1].astype(jnp.int32).reshape(-1)
    w_tbl = table_col[..., 2]
    filled = (row_tbl >= 0).reshape(-1)

    picked = jnp.take(group, src_row, axis=0)
    outgoing = jnp.where(filled[:, None], picked, jnp.zeros((), jnp.bfloat16))

    arrived = lax.all_to_all(outgoing, "rep", split_axis=0, concat_axis=0, tiled=True)
    results = run_expert(arrived, w_gate, w_up, w_down)
    returned = lax.all_to_all(results, "rep", split_axis=0, concat_axis=0, tiled=True)
    returned = returned.reshape(n_rep, n_exp, cap, width)
    after = returned[0, 0, 0, 0].astype(jnp.float32) * 0
    table_post = table_col + after
    key = table_post[..., 0].astype(jnp.int32).reshape(-1)
    w_key = table_post[..., 2].reshape(-1)
    pick = jnp.arange(micro, dtype=jnp.int32)[:, None] == key[None, :]
    mix = jnp.where(pick, w_key[None, :], 0.0).astype(jnp.bfloat16)
    partial = jnp.dot(mix, returned.reshape(slots, width), preferred_element_type=jnp.float32)
    mixed = lax.psum_scatter(partial.astype(jnp.bfloat16), "exp", scatter_dimension=0, tiled=True)
    return mixed


def solution(mesh):
    placed = (
        P(("rep", "exp"), None),
        P(("rep", "exp")),
        P(("rep", "exp"), None),
        P(("rep", "exp"), None),
        P(("rep", "exp")),
        P(),
        P(("rep", "exp"), None, None),
        P(("rep", "exp"), None, None),
        P(("rep", "exp"), None, None),
    )
    return jax.shard_map(
        shards, mesh=mesh, in_specs=placed, out_specs=P(("rep", "exp"), None), check_vma=False
    )
```

```python
import jax
import jax.numpy as jnp
from jax import lax
from jax.sharding import PartitionSpec as P


def run_expert(arrived, w_gate, w_up, w_down):
    gate_val = jnp.dot(arrived, w_gate[0], preferred_element_type=jnp.float32)
    up_val = jnp.dot(arrived, w_up[0], preferred_element_type=jnp.float32)
    act = (jax.nn.silu(gate_val) * up_val).astype(jnp.bfloat16)
    return jnp.dot(act, w_down[0], preferred_element_type=jnp.float32).astype(jnp.bfloat16)


def shards(hidden, parents, routes, gates, counts, norm_gain, w_gate, w_up, w_down):
    rows = hidden.shape[0]
    width = hidden.shape[1]
    top = routes.shape[1]
    n_rep = lax.axis_size("rep")
    n_exp = lax.axis_size("exp")
    n_dev = n_rep * n_exp
    cap = rows * top // n_dev + 2
    column = lax.axis_index("exp")
    micro = rows * n_exp
    per_expert = cap * n_exp
    slots = n_rep * per_expert

    live = jnp.arange(rows, dtype=jnp.int32) < counts[0]
    weights = gates / jnp.sum(gates, axis=1, keepdims=True) * live[:, None].astype(jnp.float32)
    flat = routes.reshape(-1)
    live_slot = jnp.repeat(live, top)
    onehot = (
        (flat[:, None] == jnp.arange(n_dev, dtype=jnp.int32)[None, :]) & live_slot[:, None]
    ).astype(jnp.int32)
    before = jnp.cumsum(onehot, axis=0) - onehot
    rank = jnp.sum(before * onehot, axis=1)
    position = jnp.where(live_slot, flat * cap + rank, n_dev * cap)
    slot_row = jnp.arange(rows * top, dtype=jnp.int32) // top
    match = position[:, None] == jnp.arange(n_dev * cap, dtype=jnp.int32)[None, :]
    filled_here = jnp.any(match, axis=0)
    row_here = jnp.sum(jnp.where(match, slot_row[:, None], 0), axis=0)
    parent_here = jnp.sum(jnp.where(match, jnp.repeat(parents, top)[:, None], 0), axis=0)
    w_here = jnp.sum(jnp.where(match, weights.reshape(-1)[:, None], 0.0), axis=0)
    table = jnp.stack(
        [
            jnp.where(filled_here, column * rows + row_here, -1).astype(jnp.float32),
            parent_here.astype(jnp.float32),
            w_here,
        ],
        axis=1,
    )

    own = hidden.astype(jnp.float32)
    own_scale = lax.rsqrt(jnp.mean(own * own, axis=1, keepdims=True) + 1e-06)
    normed = (own * own_scale * norm_gain).astype(jnp.bfloat16)
    group = lax.all_gather(normed, "exp", axis=0, tiled=True)
    table_all = lax.all_gather(table.reshape(n_rep, n_exp, cap, 3), "exp", axis=1, tiled=False)
    table_col = lax.dynamic_index_in_dim(table_all, column, axis=2, keepdims=False)
    row_tbl = table_col[..., 0].astype(jnp.int32)
    src_row = table_col[..., 1].astype(jnp.int32).reshape(-1)
    w_tbl = table_col[..., 2]
    filled = (row_tbl >= 0).reshape(-1)

    picked = jnp.take(group, src_row, axis=0)
    outgoing = jnp.where(filled[:, None], picked, jnp.zeros((), jnp.bfloat16))

    arrived = lax.all_to_all(outgoing, "rep", split_axis=0, concat_axis=0, tiled=True)
    results = run_expert(arrived, w_gate, w_up, w_down)
    returned = lax.all_to_all(results, "rep", split_axis=0, concat_axis=0, tiled=True)
    after = returned[0, 0].astype(jnp.float32) * 0
    table_post = table_col + after
    key = table_post[..., 0].astype(jnp.int32).reshape(-1)
    w_key = table_post[..., 2].reshape(-1)
    pick = jnp.arange(micro, dtype=jnp.int32)[:, None] == key[None, :]
    mix = jnp.where(pick, w_key[None, :], 0.0).astype(jnp.bfloat16)
    partial = jnp.dot(mix, returned, preferred_element_type=jnp.float32)
    mixed = lax.psum_scatter(partial.astype(jnp.bfloat16), "exp", scatter_dimension=0, tiled=True)
    return mixed


def solution(mesh):
    placed = (
        P(("rep", "exp"), None),
        P(("rep", "exp")),
        P(("rep", "exp"), None),
        P(("rep", "exp"), None),
        P(("rep", "exp")),
        P(),
        P(("rep", "exp"), None, None),
        P(("rep", "exp"), None, None),
        P(("rep", "exp"), None, None),
    )
    return jax.shard_map(
        shards, mesh=mesh, in_specs=placed, out_specs=P(("rep", "exp"), None), check_vma=False
    )
```

```python
import jax
import jax.numpy as jnp
from jax import lax
from jax.sharding import PartitionSpec as P


def run_expert(arrived, w_gate, w_up, w_down):
    gate_val = jnp.dot(arrived, w_gate[0], preferred_element_type=jnp.float32)
    up_val = jnp.dot(arrived, w_up[0], preferred_element_type=jnp.float32)
    act = (jax.nn.silu(gate_val) * up_val).astype(jnp.bfloat16)
    return jnp.dot(act, w_down[0], preferred_element_type=jnp.float32).astype(jnp.bfloat16)


def shards(hidden, parents, routes, gates, counts, norm_gain, w_gate, w_up, w_down):
    rows = hidden.shape[0]
    width = hidden.shape[1]
    top = routes.shape[1]
    n_rep = lax.axis_size("rep")
    n_exp = lax.axis_size("exp")
    n_dev = n_rep * n_exp
    cap = rows * top // n_dev + 2
    column = lax.axis_index("exp")
    micro = rows * n_exp
    per_expert = cap * n_exp
    slots = n_rep * per_expert

    live = jnp.arange(rows, dtype=jnp.int32) < counts[0]
    weights = gates / jnp.sum(gates, axis=1, keepdims=True) * live[:, None].astype(jnp.float32)
    flat = routes.reshape(-1)
    live_slot = jnp.repeat(live, top)
    onehot = (
        (flat[:, None] == jnp.arange(n_dev, dtype=jnp.int32)[None, :]) & live_slot[:, None]
    ).astype(jnp.int32)
    before = jnp.cumsum(onehot, axis=0) - onehot
    rank = jnp.sum(before * onehot, axis=1)
    position = jnp.where(live_slot, flat * cap + rank, n_dev * cap)
    slot_row = jnp.arange(rows * top, dtype=jnp.int32) // top
    match = position[:, None] == jnp.arange(n_dev * cap, dtype=jnp.int32)[None, :]
    filled_here = jnp.any(match, axis=0)
    row_here = jnp.sum(jnp.where(match, slot_row[:, None], 0), axis=0)
    parent_here = jnp.sum(jnp.where(match, jnp.repeat(parents, top)[:, None], 0), axis=0)
    w_here = jnp.sum(jnp.where(match, weights.reshape(-1)[:, None], 0.0), axis=0)
    table = jnp.stack(
        [
            jnp.where(filled_here, column * rows + row_here, -1).astype(jnp.float32),
            parent_here.astype(jnp.float32),
            w_here,
        ],
        axis=1,
    )

    own = hidden.astype(jnp.float32)
    own_scale = lax.rsqrt(jnp.mean(own * own, axis=1, keepdims=True) + 1e-06)
    normed = (own * own_scale * norm_gain).astype(jnp.bfloat16)
    table_all = lax.all_gather(table.reshape(n_rep, n_exp, cap, 3), "exp", axis=1, tiled=False)
    table_col = lax.dynamic_index_in_dim(table_all, column, axis=2, keepdims=False)
    src_row = table_col[..., 1].astype(jnp.int32).reshape(-1)

    half = width // 2
    sent = []
    order = 0
    for part in range(2):
        group = lax.all_gather(normed[:, part * half : (part + 1) * half], "exp", axis=0, tiled=True)
        picked = jnp.take(group, src_row + order, axis=0)
        sent.append(lax.all_to_all(picked, "rep", split_axis=0, concat_axis=0, tiled=True))
        order = (sent[-1][0, 0] * 0).astype(jnp.int32)
    gate_val = jnp.dot(sent[0], w_gate[0, :half], preferred_element_type=jnp.float32)
    gate_val = gate_val + jnp.dot(sent[1], w_gate[0, half:], preferred_element_type=jnp.float32)
    up_val = jnp.dot(sent[0], w_up[0, :half], preferred_element_type=jnp.float32)
    up_val = up_val + jnp.dot(sent[1], w_up[0, half:], preferred_element_type=jnp.float32)
    act = (jax.nn.silu(gate_val) * up_val).astype(jnp.bfloat16)
    mixed = []
    hold = 0.0
    for part in range(2):
        results = jnp.dot(act, w_down[0, :, part * half : (part + 1) * half], preferred_element_type=jnp.float32)
        results = (results + hold).astype(jnp.bfloat16)
        returned = lax.all_to_all(results, "rep", split_axis=0, concat_axis=0, tiled=True)
        after = returned[0, 0].astype(jnp.float32) * 0
        table_post = table_col + after
        key = table_post[..., 0].astype(jnp.int32).reshape(-1)
        w_key = table_post[..., 2].reshape(-1)
        pick = jnp.arange(micro, dtype=jnp.int32)[:, None] == key[None, :]
        mix = jnp.where(pick, w_key[None, :], 0.0).astype(jnp.bfloat16)
        partial = jnp.dot(mix, returned, preferred_element_type=jnp.float32)
        hold = partial[0, 0] * 0
        mixed.append(
            lax.psum_scatter(partial.astype(jnp.bfloat16), "exp", scatter_dimension=0, tiled=True)
        )
    return jnp.concatenate(mixed, axis=1)


def solution(mesh):
    placed = (
        P(("rep", "exp"), None),
        P(("rep", "exp")),
        P(("rep", "exp"), None),
        P(("rep", "exp"), None),
        P(("rep", "exp")),
        P(),
        P(("rep", "exp"), None, None),
        P(("rep", "exp"), None, None),
        P(("rep", "exp"), None, None),
    )
    return jax.shard_map(
        shards, mesh=mesh, in_specs=placed, out_specs=P(("rep", "exp"), None), check_vma=False
    )
```

```python
import jax
import jax.numpy as jnp
from jax import lax
from jax.sharding import PartitionSpec as P


def run_expert(arrived, w_gate, w_up, w_down):
    gate_val = jnp.dot(arrived, w_gate[0], preferred_element_type=jnp.float32)
    up_val = jnp.dot(arrived, w_up[0], preferred_element_type=jnp.float32)
    act = (jax.nn.silu(gate_val) * up_val).astype(jnp.bfloat16)
    return jnp.dot(act, w_down[0], preferred_element_type=jnp.float32).astype(jnp.bfloat16)


def shards(hidden, parents, routes, gates, counts, norm_gain, w_gate, w_up, w_down):
    rows = hidden.shape[0]
    width = hidden.shape[1]
    top = routes.shape[1]
    n_rep = lax.axis_size("rep")
    n_exp = lax.axis_size("exp")
    n_dev = n_rep * n_exp
    cap = rows * top // n_dev + 2
    column = lax.axis_index("exp")
    micro = rows * n_exp
    per_expert = cap * n_exp
    slots = n_rep * per_expert

    live = jnp.arange(rows, dtype=jnp.int32) < counts[0]
    weights = gates / jnp.sum(gates, axis=1, keepdims=True) * live[:, None].astype(jnp.float32)
    flat = routes.reshape(-1)
    live_slot = jnp.repeat(live, top)
    onehot = (
        (flat[:, None] == jnp.arange(n_dev, dtype=jnp.int32)[None, :]) & live_slot[:, None]
    ).astype(jnp.int32)
    before = jnp.cumsum(onehot, axis=0) - onehot
    rank = jnp.sum(before * onehot, axis=1)
    position = jnp.where(live_slot, flat * cap + rank, n_dev * cap)
    slot_row = jnp.arange(rows * top, dtype=jnp.int32) // top
    match = position[:, None] == jnp.arange(n_dev * cap, dtype=jnp.int32)[None, :]
    filled_here = jnp.any(match, axis=0)
    row_here = jnp.sum(jnp.where(match, slot_row[:, None], 0), axis=0)
    parent_here = jnp.sum(jnp.where(match, jnp.repeat(parents, top)[:, None], 0), axis=0)
    w_here = jnp.sum(jnp.where(match, weights.reshape(-1)[:, None], 0.0), axis=0)
    table = jnp.stack(
        [
            jnp.where(filled_here, column * rows + row_here, -1).astype(jnp.float32),
            parent_here.astype(jnp.float32),
            w_here,
        ],
        axis=1,
    )

    own = hidden.astype(jnp.float32)
    own_scale = lax.rsqrt(jnp.mean(own * own, axis=1, keepdims=True) + 1e-06)
    normed = (own * own_scale * norm_gain).astype(jnp.bfloat16)
    group = lax.all_gather(normed, "exp", axis=0, tiled=True)
    table_all = lax.all_gather(table.reshape(n_rep, n_exp, cap, 3), "exp", axis=1, tiled=False)
    table_col = lax.dynamic_index_in_dim(table_all, column, axis=2, keepdims=False)
    row_tbl = table_col[..., 0].astype(jnp.int32)
    src_row = table_col[..., 1].astype(jnp.int32).reshape(-1)
    w_tbl = table_col[..., 2]
    filled = (row_tbl >= 0).reshape(-1)

    src_key = jnp.where(filled, src_row, -1)
    choose = (src_key[:, None] == jnp.arange(micro, dtype=jnp.int32)[None, :]).astype(jnp.bfloat16)
    outgoing = jnp.dot(choose, group, preferred_element_type=jnp.float32).astype(jnp.bfloat16)

    arrived = lax.all_to_all(outgoing, "rep", split_axis=0, concat_axis=0, tiled=True)
    results = run_expert(arrived, w_gate, w_up, w_down)
    returned = lax.all_to_all(results, "rep", split_axis=0, concat_axis=0, tiled=True)
    after = returned[0, 0].astype(jnp.float32) * 0
    table_post = table_col + after
    key = table_post[..., 0].astype(jnp.int32).reshape(-1)
    w_key = table_post[..., 2].reshape(-1)
    pick = jnp.arange(micro, dtype=jnp.int32)[:, None] == key[None, :]
    mix = jnp.where(pick, w_key[None, :], 0.0).astype(jnp.bfloat16)
    partial = jnp.dot(mix, returned, preferred_element_type=jnp.float32)
    mixed = lax.psum_scatter(partial.astype(jnp.bfloat16), "exp", scatter_dimension=0, tiled=True)
    return mixed


def solution(mesh):
    placed = (
        P(("rep", "exp"), None),
        P(("rep", "exp")),
        P(("rep", "exp"), None),
        P(("rep", "exp"), None),
        P(("rep", "exp")),
        P(),
        P(("rep", "exp"), None, None),
        P(("rep", "exp"), None, None),
        P(("rep", "exp"), None, None),
    )
    return jax.shard_map(
        shards, mesh=mesh, in_specs=placed, out_specs=P(("rep", "exp"), None), check_vma=False
    )
```

```python
import jax
import jax.numpy as jnp
from jax import lax
from jax.sharding import PartitionSpec as P


def run_expert(arrived, w_gate, w_up, w_down):
    gate_val = jnp.dot(arrived, w_gate[0], preferred_element_type=jnp.float32)
    up_val = jnp.dot(arrived, w_up[0], preferred_element_type=jnp.float32)
    act = (jax.nn.silu(gate_val) * up_val).astype(jnp.bfloat16)
    return jnp.dot(act, w_down[0], preferred_element_type=jnp.float32).astype(jnp.bfloat16)


def shards(hidden, parents, routes, gates, counts, norm_gain, w_gate, w_up, w_down):
    rows = hidden.shape[0]
    width = hidden.shape[1]
    top = routes.shape[1]
    n_rep = lax.axis_size("rep")
    n_exp = lax.axis_size("exp")
    n_dev = n_rep * n_exp
    cap = rows * top // n_dev + 2
    column = lax.axis_index("exp")
    micro = rows * n_exp
    per_expert = cap * n_exp
    slots = n_rep * per_expert

    live = jnp.arange(rows, dtype=jnp.int32) < counts[0]
    weights = gates / jnp.sum(gates, axis=1, keepdims=True) * live[:, None].astype(jnp.float32)
    flat = routes.reshape(-1)
    live_slot = jnp.repeat(live, top)
    onehot = (
        (flat[:, None] == jnp.arange(n_dev, dtype=jnp.int32)[None, :]) & live_slot[:, None]
    ).astype(jnp.int32)
    before = jnp.cumsum(onehot, axis=0) - onehot
    rank = jnp.sum(before * onehot, axis=1)
    position = jnp.where(live_slot, flat * cap + rank, n_dev * cap)
    slot_row = jnp.arange(rows * top, dtype=jnp.int32) // top
    match = position[:, None] == jnp.arange(n_dev * cap, dtype=jnp.int32)[None, :]
    filled_here = jnp.any(match, axis=0)
    row_here = jnp.sum(jnp.where(match, slot_row[:, None], 0), axis=0)
    parent_here = jnp.sum(jnp.where(match, jnp.repeat(parents, top)[:, None], 0), axis=0)
    w_here = jnp.sum(jnp.where(match, weights.reshape(-1)[:, None], 0.0), axis=0)
    table = jnp.stack(
        [
            jnp.where(filled_here, column * rows + row_here, -1).astype(jnp.float32),
            parent_here.astype(jnp.float32),
            w_here,
        ],
        axis=1,
    )

    own = hidden.astype(jnp.float32)
    own_scale = lax.rsqrt(jnp.mean(own * own, axis=1, keepdims=True) + 1e-06)
    normed = (own * own_scale * norm_gain).astype(jnp.bfloat16)
    group = lax.all_gather(normed, "exp", axis=0, tiled=True)
    table_all = lax.all_gather(table.reshape(n_rep, n_exp, cap, 3), "exp", axis=1, tiled=False)
    table_col = lax.dynamic_index_in_dim(table_all, column, axis=2, keepdims=False)
    row_tbl = table_col[..., 0].astype(jnp.int32)
    src_row = table_col[..., 1].astype(jnp.int32).reshape(-1)
    w_tbl = table_col[..., 2]
    filled = (row_tbl >= 0).reshape(-1)

    src_key = jnp.where(filled, src_row, -1)
    choose = (src_key[:, None] == jnp.arange(micro, dtype=jnp.int32)[None, :]).astype(jnp.bfloat16)
    key = table_col[..., 0].astype(jnp.int32).reshape(-1)
    w_key = table_col[..., 2].reshape(-1)
    pick = jnp.arange(micro, dtype=jnp.int32)[:, None] == key[None, :]
    mix = jnp.where(pick, w_key[None, :], 0.0).astype(jnp.bfloat16)
    outgoing = jnp.dot(choose, group, preferred_element_type=jnp.float32) + jnp.sum(mix) * 0
    outgoing = outgoing.astype(jnp.bfloat16)

    arrived = lax.all_to_all(outgoing, "rep", split_axis=0, concat_axis=0, tiled=True)
    results = run_expert(arrived, w_gate, w_up, w_down)
    results = results + jnp.sum(mix) * 0
    returned = lax.all_to_all(results, "rep", split_axis=0, concat_axis=0, tiled=True)
    partial = jnp.dot(mix, returned, preferred_element_type=jnp.float32)
    mixed = lax.psum_scatter(partial.astype(jnp.bfloat16), "exp", scatter_dimension=0, tiled=True)
    return mixed


def solution(mesh):
    placed = (
        P(("rep", "exp"), None),
        P(("rep", "exp")),
        P(("rep", "exp"), None),
        P(("rep", "exp"), None),
        P(("rep", "exp")),
        P(),
        P(("rep", "exp"), None, None),
        P(("rep", "exp"), None, None),
        P(("rep", "exp"), None, None),
    )
    return jax.shard_map(
        shards, mesh=mesh, in_specs=placed, out_specs=P(("rep", "exp"), None), check_vma=False
    )
```

```python
import jax
import jax.numpy as jnp
from jax import lax
from jax.sharding import PartitionSpec as P


def run_expert(arrived, w_gate, w_up, w_down):
    gate_val = jnp.dot(arrived, w_gate[0], preferred_element_type=jnp.float32)
    up_val = jnp.dot(arrived, w_up[0], preferred_element_type=jnp.float32)
    act = (jax.nn.silu(gate_val) * up_val).astype(jnp.bfloat16)
    return jnp.dot(act, w_down[0], preferred_element_type=jnp.float32).astype(jnp.bfloat16)


def shards(hidden, parents, routes, gates, counts, norm_gain, w_gate, w_up, w_down):
    rows = hidden.shape[0]
    width = hidden.shape[1]
    top = routes.shape[1]
    n_rep = lax.axis_size("rep")
    n_exp = lax.axis_size("exp")
    n_dev = n_rep * n_exp
    cap = rows * top // n_dev + 2
    column = lax.axis_index("exp")
    micro = rows * n_exp
    per_expert = cap * n_exp
    slots = n_rep * per_expert

    live = jnp.arange(rows, dtype=jnp.int32) < counts[0]
    weights = gates / jnp.sum(gates, axis=1, keepdims=True) * live[:, None].astype(jnp.float32)
    flat = routes.reshape(-1)
    live_slot = jnp.repeat(live, top)
    onehot = (
        (flat[:, None] == jnp.arange(n_dev, dtype=jnp.int32)[None, :]) & live_slot[:, None]
    ).astype(jnp.int32)
    before = jnp.cumsum(onehot, axis=0) - onehot
    rank = jnp.sum(before * onehot, axis=1)
    position = jnp.where(live_slot, flat * cap + rank, n_dev * cap)
    slot_row = jnp.arange(rows * top, dtype=jnp.int32) // top
    match = position[:, None] == jnp.arange(n_dev * cap, dtype=jnp.int32)[None, :]
    filled_here = jnp.any(match, axis=0)
    row_here = jnp.sum(jnp.where(match, slot_row[:, None], 0), axis=0)
    parent_here = jnp.sum(jnp.where(match, jnp.repeat(parents, top)[:, None], 0), axis=0)
    w_here = jnp.sum(jnp.where(match, weights.reshape(-1)[:, None], 0.0), axis=0)
    table = jnp.stack(
        [
            jnp.where(filled_here, column * rows + row_here, -1).astype(jnp.float32),
            parent_here.astype(jnp.float32),
            w_here,
        ],
        axis=1,
    )

    own = hidden.astype(jnp.float32)
    own_scale = lax.rsqrt(jnp.mean(own * own, axis=1, keepdims=True) + 1e-06)
    normed = (own * own_scale * norm_gain).astype(jnp.bfloat16)
    group = lax.all_gather(normed, "exp", axis=0, tiled=True)
    table_all = lax.all_gather(table.reshape(n_rep, n_exp, cap, 3), "exp", axis=1, tiled=False)
    table_col = lax.dynamic_index_in_dim(table_all, column, axis=2, keepdims=False)
    row_tbl = table_col[..., 0].astype(jnp.int32)
    src_row = table_col[..., 1].astype(jnp.int32).reshape(-1)
    w_tbl = table_col[..., 2]
    filled = (row_tbl >= 0).reshape(-1)

    src_key = jnp.where(filled, src_row, -1)
    choose = (src_key[:, None] == jnp.arange(micro, dtype=jnp.int32)[None, :]).astype(jnp.bfloat16)
    choose = lax.optimization_barrier(choose)
    key = table_col[..., 0].astype(jnp.int32).reshape(-1)
    w_key = table_col[..., 2].reshape(-1)
    pick = jnp.arange(micro, dtype=jnp.int32)[:, None] == key[None, :]
    mix = jnp.where(pick, w_key[None, :], 0.0).astype(jnp.bfloat16)
    outgoing = jnp.dot(choose, group, preferred_element_type=jnp.float32) + jnp.sum(mix) * 0
    outgoing = outgoing.astype(jnp.bfloat16)

    arrived = lax.all_to_all(outgoing, "rep", split_axis=0, concat_axis=0, tiled=True)
    results = run_expert(arrived, w_gate, w_up, w_down)
    results = results + jnp.sum(mix) * 0
    returned = lax.all_to_all(results, "rep", split_axis=0, concat_axis=0, tiled=True)
    partial = jnp.dot(mix, returned, preferred_element_type=jnp.float32)
    mixed = lax.psum_scatter(partial.astype(jnp.bfloat16), "exp", scatter_dimension=0, tiled=True)
    return mixed


def solution(mesh):
    placed = (
        P(("rep", "exp"), None),
        P(("rep", "exp")),
        P(("rep", "exp"), None),
        P(("rep", "exp"), None),
        P(("rep", "exp")),
        P(),
        P(("rep", "exp"), None, None),
        P(("rep", "exp"), None, None),
        P(("rep", "exp"), None, None),
    )
    return jax.shard_map(
        shards, mesh=mesh, in_specs=placed, out_specs=P(("rep", "exp"), None), check_vma=False
    )
```

```python
import jax
import jax.numpy as jnp
from jax import lax
from jax.sharding import PartitionSpec as P


def run_expert(arrived, w_gate, w_up, w_down):
    ffw = w_gate.shape[2]
    both = jnp.concatenate([w_gate[0], w_up[0]], axis=1)
    joint = jnp.dot(arrived, both, preferred_element_type=jnp.float32)
    gate_val = joint[:, :ffw]
    up_val = joint[:, ffw:]
    act = (jax.nn.silu(gate_val) * up_val).astype(jnp.bfloat16)
    return jnp.dot(act, w_down[0], preferred_element_type=jnp.float32).astype(jnp.bfloat16)


def shards(hidden, parents, routes, gates, counts, norm_gain, w_gate, w_up, w_down):
    rows = hidden.shape[0]
    width = hidden.shape[1]
    top = routes.shape[1]
    n_rep = lax.axis_size("rep")
    n_exp = lax.axis_size("exp")
    n_dev = n_rep * n_exp
    cap = rows * top // n_dev + 2
    column = lax.axis_index("exp")
    micro = rows * n_exp
    per_expert = cap * n_exp
    slots = n_rep * per_expert

    live = jnp.arange(rows, dtype=jnp.int32) < counts[0]
    weights = gates / jnp.sum(gates, axis=1, keepdims=True) * live[:, None].astype(jnp.float32)
    flat = routes.reshape(-1)
    live_slot = jnp.repeat(live, top)
    onehot = (
        (flat[:, None] == jnp.arange(n_dev, dtype=jnp.int32)[None, :]) & live_slot[:, None]
    ).astype(jnp.int32)
    before = jnp.cumsum(onehot, axis=0) - onehot
    rank = jnp.sum(before * onehot, axis=1)
    position = jnp.where(live_slot, flat * cap + rank, n_dev * cap)
    slot_row = jnp.arange(rows * top, dtype=jnp.int32) // top
    match = position[:, None] == jnp.arange(n_dev * cap, dtype=jnp.int32)[None, :]
    filled_here = jnp.any(match, axis=0)
    row_here = jnp.sum(jnp.where(match, slot_row[:, None], 0), axis=0)
    parent_here = jnp.sum(jnp.where(match, jnp.repeat(parents, top)[:, None], 0), axis=0)
    w_here = jnp.sum(jnp.where(match, weights.reshape(-1)[:, None], 0.0), axis=0)
    table = jnp.stack(
        [
            jnp.where(filled_here, column * rows + row_here, -1).astype(jnp.float32),
            parent_here.astype(jnp.float32),
            w_here,
        ],
        axis=1,
    )

    own = hidden.astype(jnp.float32)
    own_scale = lax.rsqrt(jnp.mean(own * own, axis=1, keepdims=True) + 1e-06)
    normed = (own * own_scale * norm_gain).astype(jnp.bfloat16)
    group = lax.all_gather(normed, "exp", axis=0, tiled=True)
    table_all = lax.all_gather(table.reshape(n_rep, n_exp, cap, 3), "exp", axis=1, tiled=False)
    table_col = lax.dynamic_index_in_dim(table_all, column, axis=2, keepdims=False)
    row_tbl = table_col[..., 0].astype(jnp.int32)
    src_row = table_col[..., 1].astype(jnp.int32).reshape(-1)
    w_tbl = table_col[..., 2]
    filled = (row_tbl >= 0).reshape(-1)

    src_key = jnp.where(filled, src_row, -1)
    choose = (src_key[:, None] == jnp.arange(micro, dtype=jnp.int32)[None, :]).astype(jnp.bfloat16)
    choose = lax.optimization_barrier(choose)
    key = table_col[..., 0].astype(jnp.int32).reshape(-1)
    w_key = table_col[..., 2].reshape(-1)
    pick = jnp.arange(micro, dtype=jnp.int32)[:, None] == key[None, :]
    mix = jnp.where(pick, w_key[None, :], 0.0).astype(jnp.bfloat16)
    outgoing = jnp.dot(choose, group, preferred_element_type=jnp.float32) + jnp.sum(mix) * 0
    outgoing = outgoing.astype(jnp.bfloat16)

    arrived = lax.all_to_all(outgoing, "rep", split_axis=0, concat_axis=0, tiled=True)
    results = run_expert(arrived, w_gate, w_up, w_down)
    results = results + jnp.sum(mix) * 0
    returned = lax.all_to_all(results, "rep", split_axis=0, concat_axis=0, tiled=True)
    partial = jnp.dot(mix, returned, preferred_element_type=jnp.float32)
    mixed = lax.psum_scatter(partial.astype(jnp.bfloat16), "exp", scatter_dimension=0, tiled=True)
    return mixed


def solution(mesh):
    placed = (
        P(("rep", "exp"), None),
        P(("rep", "exp")),
        P(("rep", "exp"), None),
        P(("rep", "exp"), None),
        P(("rep", "exp")),
        P(),
        P(("rep", "exp"), None, None),
        P(("rep", "exp"), None, None),
        P(("rep", "exp"), None, None),
    )
    return jax.shard_map(
        shards, mesh=mesh, in_specs=placed, out_specs=P(("rep", "exp"), None), check_vma=False
    )
```

```python
import jax
import jax.numpy as jnp
from jax import lax
from jax.sharding import PartitionSpec as P


def run_expert(arrived, w_gate, w_up, w_down):
    gate_val = jnp.dot(arrived, w_gate[0], preferred_element_type=jnp.float32)
    up_val = jnp.dot(arrived, w_up[0], preferred_element_type=jnp.float32)
    act = (jax.nn.silu(gate_val) * up_val).astype(jnp.bfloat16)
    return jnp.dot(act, w_down[0], preferred_element_type=jnp.float32).astype(jnp.bfloat16)


def shards(hidden, parents, routes, gates, counts, norm_gain, w_gate, w_up, w_down):
    rows = hidden.shape[0]
    width = hidden.shape[1]
    top = routes.shape[1]
    n_rep = lax.axis_size("rep")
    n_exp = lax.axis_size("exp")
    n_dev = n_rep * n_exp
    cap = rows * top // n_dev + 2
    column = lax.axis_index("exp")
    micro = rows * n_exp
    per_expert = cap * n_exp
    slots = n_rep * per_expert

    live = jnp.arange(rows, dtype=jnp.int32) < counts[0]
    weights = gates / jnp.sum(gates, axis=1, keepdims=True) * live[:, None].astype(jnp.float32)
    flat = routes.reshape(-1)
    live_slot = jnp.repeat(live, top)
    onehot = (
        (flat[:, None] == jnp.arange(n_dev, dtype=jnp.int32)[None, :]) & live_slot[:, None]
    ).astype(jnp.int32)
    before = jnp.cumsum(onehot, axis=0) - onehot
    rank = jnp.sum(before * onehot, axis=1)
    position = jnp.where(live_slot, flat * cap + rank, n_dev * cap)
    slot_row = jnp.arange(rows * top, dtype=jnp.int32) // top
    match = position[:, None] == jnp.arange(n_dev * cap, dtype=jnp.int32)[None, :]
    filled_here = jnp.any(match, axis=0)
    row_here = jnp.sum(jnp.where(match, slot_row[:, None], 0), axis=0)
    parent_here = jnp.sum(jnp.where(match, jnp.repeat(parents, top)[:, None], 0), axis=0)
    w_here = jnp.sum(jnp.where(match, weights.reshape(-1)[:, None], 0.0), axis=0)
    table = jnp.stack(
        [
            jnp.where(filled_here, column * rows + row_here, -1).astype(jnp.float32),
            parent_here.astype(jnp.float32),
            w_here,
        ],
        axis=1,
    )

    group = lax.all_gather(hidden, "exp", axis=0, tiled=True)
    own = hidden.astype(jnp.float32)
    own_scale = lax.rsqrt(jnp.mean(own * own, axis=1) + 1e-06)
    scale_all = lax.all_gather(own_scale, "exp", axis=0, tiled=True)
    table_all = lax.all_gather(table.reshape(n_rep, n_exp, cap, 3), "exp", axis=1, tiled=False)
    table_col = lax.dynamic_index_in_dim(table_all, column, axis=2, keepdims=False)
    row_tbl = table_col[..., 0].astype(jnp.int32)
    src_row = table_col[..., 1].astype(jnp.int32).reshape(-1)
    w_tbl = table_col[..., 2]
    filled = (row_tbl >= 0).reshape(-1)

    src_key = jnp.where(filled, src_row, -1)
    choose = (src_key[:, None] == jnp.arange(micro, dtype=jnp.int32)[None, :]).astype(jnp.bfloat16)
    choose = lax.optimization_barrier(choose)
    key = table_col[..., 0].astype(jnp.int32).reshape(-1)
    w_key = table_col[..., 2].reshape(-1)
    pick = jnp.arange(micro, dtype=jnp.int32)[:, None] == key[None, :]
    mix = jnp.where(pick, w_key[None, :], 0.0).astype(jnp.bfloat16)
    scale_sel = jnp.take(scale_all, jnp.maximum(src_key, 0))
    picked = jnp.dot(choose, group, preferred_element_type=jnp.float32)
    outgoing = picked * scale_sel[:, None] * norm_gain + jnp.sum(mix) * 0
    outgoing = outgoing.astype(jnp.bfloat16)

    arrived = lax.all_to_all(outgoing, "rep", split_axis=0, concat_axis=0, tiled=True)
    results = run_expert(arrived, w_gate, w_up, w_down)
    results = results + jnp.sum(mix) * 0
    returned = lax.all_to_all(results, "rep", split_axis=0, concat_axis=0, tiled=True)
    partial = jnp.dot(mix, returned, preferred_element_type=jnp.float32)
    mixed = lax.psum_scatter(partial.astype(jnp.bfloat16), "exp", scatter_dimension=0, tiled=True)
    return mixed


def solution(mesh):
    placed = (
        P(("rep", "exp"), None),
        P(("rep", "exp")),
        P(("rep", "exp"), None),
        P(("rep", "exp"), None),
        P(("rep", "exp")),
        P(),
        P(("rep", "exp"), None, None),
        P(("rep", "exp"), None, None),
        P(("rep", "exp"), None, None),
    )
    return jax.shard_map(
        shards, mesh=mesh, in_specs=placed, out_specs=P(("rep", "exp"), None), check_vma=False
    )
```

```python
import jax
import jax.numpy as jnp
from jax import lax
from jax.sharding import PartitionSpec as P


def run_expert(arrived, w_gate, w_up, w_down):
    gate_val = jnp.dot(arrived, w_gate[0], preferred_element_type=jnp.float32)
    up_val = jnp.dot(arrived, w_up[0], preferred_element_type=jnp.float32)
    act = (jax.nn.silu(gate_val) * up_val).astype(jnp.bfloat16)
    return jnp.dot(act, w_down[0], preferred_element_type=jnp.float32).astype(jnp.bfloat16)


def shards(hidden, parents, routes, gates, counts, norm_gain, w_gate, w_up, w_down):
    rows = hidden.shape[0]
    width = hidden.shape[1]
    top = routes.shape[1]
    n_rep = lax.axis_size("rep")
    n_exp = lax.axis_size("exp")
    n_dev = n_rep * n_exp
    cap = rows * top // n_dev + 2
    column = lax.axis_index("exp")
    micro = rows * n_exp
    per_expert = cap * n_exp
    slots = n_rep * per_expert

    live = jnp.arange(rows, dtype=jnp.int32) < counts[0]
    weights = gates / jnp.sum(gates, axis=1, keepdims=True) * live[:, None].astype(jnp.float32)
    flat = routes.reshape(-1)
    live_slot = jnp.repeat(live, top)
    onehot = (
        (flat[:, None] == jnp.arange(n_dev, dtype=jnp.int32)[None, :]) & live_slot[:, None]
    ).astype(jnp.int32)
    before = jnp.cumsum(onehot, axis=0) - onehot
    rank = jnp.sum(before * onehot, axis=1)
    position = jnp.where(live_slot, flat * cap + rank, n_dev * cap)
    slot_row = jnp.arange(rows * top, dtype=jnp.int32) // top
    match = position[:, None] == jnp.arange(n_dev * cap, dtype=jnp.int32)[None, :]
    filled_here = jnp.any(match, axis=0)
    row_here = jnp.sum(jnp.where(match, slot_row[:, None], 0), axis=0)
    parent_here = jnp.sum(jnp.where(match, jnp.repeat(parents, top)[:, None], 0), axis=0)
    w_here = jnp.sum(jnp.where(match, weights.reshape(-1)[:, None], 0.0), axis=0)
    group = lax.all_gather(hidden, "exp", axis=0, tiled=True)
    own = hidden.astype(jnp.float32)
    own_scale = lax.rsqrt(jnp.mean(own * own, axis=1) + 1e-06)
    table = jnp.stack(
        [
            jnp.where(filled_here, column * rows + row_here, -1).astype(jnp.float32),
            parent_here.astype(jnp.float32),
            w_here,
            jnp.pad(own_scale, (0, n_dev * cap - rows)),
        ],
        axis=1,
    )
    table_all = lax.all_gather(table.reshape(n_rep, n_exp, cap, 4), "exp", axis=1, tiled=False)
    scale_all = jnp.transpose(table_all[..., 3], (1, 0, 2, 3)).reshape(n_exp, -1)[:, :rows].reshape(-1)
    table_col = lax.dynamic_index_in_dim(table_all, column, axis=2, keepdims=False)
    row_tbl = table_col[..., 0].astype(jnp.int32)
    src_row = table_col[..., 1].astype(jnp.int32).reshape(-1)
    w_tbl = table_col[..., 2]
    filled = (row_tbl >= 0).reshape(-1)

    src_key = jnp.where(filled, src_row, -1)
    choose = (src_key[:, None] == jnp.arange(micro, dtype=jnp.int32)[None, :]).astype(jnp.bfloat16)
    choose = lax.optimization_barrier(choose)
    key = table_col[..., 0].astype(jnp.int32).reshape(-1)
    w_key = table_col[..., 2].reshape(-1)
    pick = jnp.arange(micro, dtype=jnp.int32)[:, None] == key[None, :]
    mix = jnp.where(pick, w_key[None, :], 0.0).astype(jnp.bfloat16)
    scale_sel = jnp.take(scale_all, jnp.maximum(src_key, 0))
    picked = jnp.dot(choose, group, preferred_element_type=jnp.float32)
    outgoing = picked * scale_sel[:, None] * norm_gain + jnp.sum(mix) * 0
    outgoing = outgoing.astype(jnp.bfloat16)

    arrived = lax.all_to_all(outgoing, "rep", split_axis=0, concat_axis=0, tiled=True)
    results = run_expert(arrived, w_gate, w_up, w_down)
    results = results + jnp.sum(mix) * 0
    returned = lax.all_to_all(results, "rep", split_axis=0, concat_axis=0, tiled=True)
    partial = jnp.dot(mix, returned, preferred_element_type=jnp.float32)
    mixed = lax.psum_scatter(partial.astype(jnp.bfloat16), "exp", scatter_dimension=0, tiled=True)
    return mixed


def solution(mesh):
    placed = (
        P(("rep", "exp"), None),
        P(("rep", "exp")),
        P(("rep", "exp"), None),
        P(("rep", "exp"), None),
        P(("rep", "exp")),
        P(),
        P(("rep", "exp"), None, None),
        P(("rep", "exp"), None, None),
        P(("rep", "exp"), None, None),
    )
    return jax.shard_map(
        shards, mesh=mesh, in_specs=placed, out_specs=P(("rep", "exp"), None), check_vma=False
    )
```
